32 devices in a mesh: seq: 8 (over z, y), head: 4 (over x, core).
Axes of the slice: x: 2, y: 2, z: 4, core: 2. Of those that a mesh axis runs over, the one named last changes fastest.
Arguments:
- query: bfloat16 [8192, 4096], P('seq', 'head'), may hold values from -0.15625 to 0.15625
- key: bfloat16 [8192, 4096], P('seq', 'head'), may hold values from -0.15625 to 0.15625
- value: bfloat16 [8192, 4096], P('seq', 'head'), may hold values from -18 to 18, as said below
- level_coef: float32 [4, 32, 8192], P(None, 'head', 'seq'), may hold values from 0.25 to 2.5
- gain: float32 [4096], P('head'), may hold values from 0.5 to 1.5
- cotangent: bfloat16 [8192, 4096], P('seq', 'head'), may hold values from -0.625 to 0.625
Outputs:
- mixed: bfloat16 [8192, 4096], P('seq', 'head')
- grad_query: bfloat16 [8192, 4096], P('seq', 'head')
- grad_key: bfloat16 [8192, 4096], P('seq', 'head')
- grad_value: bfloat16 [8192, 4096], P('seq', 'head')
- grad_level: float32 [4, 32, 8192], P(None, 'head', 'seq')
- grad_gain: float32 [4096], P('head')
The draws below stay inside these ranges and needn't reach their ends.
Inputs may be any that keep to these rules, and one draw needn't show every extreme that they name: `value`: real values.
All inputs are finite; a program needn't handle non-finite values.
Results may differ from the reference program's by a relative error of at most 0.0065.
Values sent between devices are 32-bit elements; how exact they have to be, the bound alone decides.
No kernel may reach another device: no remote copies, remote signals or barrier semaphores. Data moves between devices by JAX's collectives and lax.ppermute only.
A program may use at most 128 MiB of HBM per device.

```python
import math
import jax
import jax.numpy as jnp
from jax import lax

HEADS = 32
HEAD_DIM = 128
TOK_DEV = 1024
TOKENS = 8192
LEVELS = 4
N_SEQ = 8


def draw_value(key, part):
    first = jax.random.fold_in(jax.random.fold_in(key, 7), 0)
    columns = jnp.arange(HEADS * HEAD_DIM, dtype=jnp.int32) // HEAD_DIM
    scale = 1.0 + 2.0 * columns.astype(jnp.float32) / max(HEADS - 1, 1)
    base = jnp.clip(jax.random.normal(first, (TOKENS, HEADS * HEAD_DIM), jnp.float32), -6.0, 6.0)
    return (base * scale[None, :]).astype(jnp.bfloat16)


def level_of(own_key, extent, cuts, low, largest):
    level = 1.0
    for position, blocks in cuts:
        heights = jax.random.uniform(jax.random.fold_in(jax.random.fold_in(own_key, 6), position), (blocks,), jnp.float32, low / len(cuts), largest / len(cuts))
        level = level * jnp.repeat(jnp.exp(heights), extent[position] // blocks).reshape((-1,) + (1,) * (len(extent) - 1 - position))
    return level


def normal_values(own_key, dims, deviation, most, pieces=(), kind=jnp.bfloat16):
    values = jax.random.normal(own_key, dims, jnp.float32) * deviation
    if len(pieces) > 0:
        values = level_of(own_key, dims, pieces, -0.22, 0.18) * values
    return jnp.clip(values, min=-most, max=most).astype(kind)


def setup_inputs(seed: int = 0) -> dict:
    key_of = jax.random.split(jax.random.key(seed), 7)
    query = normal_values(key_of[0], (TOKENS, HEADS * HEAD_DIM), 0.026, 0.15625, ((0, 8), (1, 4)))
    key = normal_values(key_of[1], (TOKENS, HEADS * HEAD_DIM), 0.026, 0.15625, ((0, 8), (1, 4)))
    value = draw_value(jax.random.fold_in(key_of[6], 71), 0)
    level_coef = jnp.clip(jnp.exp(math.log(2.5) - 2.3025851 * jax.random.uniform(key_of[3], (LEVELS, HEADS, TOKENS), jnp.float32) ** level_of(key_of[3], (LEVELS, HEADS, TOKENS), ((1, 4), (2, 8)), -0.2, 0.2)), 0.25, 2.5)
    gain = jnp.clip(1.0 + 0.1 * jax.random.normal(key_of[4], (HEADS * HEAD_DIM,), jnp.float32), 0.5, 1.5)
    cotangent = normal_values(key_of[5], (TOKENS, HEADS * HEAD_DIM), 0.1, 0.625, ((0, 8), (1, 4)))
    return {"query": query, "key": key, "value": value, "level_coef": level_coef, "gain": gain, "cotangent": cotangent}


EPS = 1e-06

def sibling_sums(states, level):
    count = states.shape[0]
    span = 2 ** level
    blocks = states.reshape((count // span, span) + states.shape[1:]).sum(axis=1)
    pairs = blocks.reshape((count // (2 * span), 2) + blocks.shape[1:])
    flipped = pairs[:, ::-1].reshape(blocks.shape)
    return jnp.repeat(flipped, span, axis=0)

def causal_scores(query, key):
    size = query.shape[0]
    scores = jnp.einsum('the,she->hts', query.astype(jnp.float32), key.astype(jnp.float32))
    causal = jnp.arange(size, dtype=jnp.int32)[:, None] >= jnp.arange(size, dtype=jnp.int32)[None, :]
    return (jnp.where(causal[None], scores, 0.0).astype(jnp.bfloat16).astype(jnp.float32), causal)

def forward_group(query, key, value, coef, buckets):
    kept, causal = causal_scores(query, key)
    local = jnp.einsum('hts,she->the', kept, value.astype(jnp.float32))
    reads = jnp.einsum('the,lhef->lthf', query.astype(jnp.float32), buckets.astype(jnp.float32))
    total = coef[0].T[:, :, None] * local
    total = total + lax.optimization_barrier(jnp.sum(coef[1:].transpose(0, 2, 1)[..., None] * reads, axis=0))
    return total

def backward_group(query, key, value, coef, buckets, grad_out):
    qf = query.astype(jnp.float32)
    kf = key.astype(jnp.float32)
    vf = value.astype(jnp.float32)
    bf = buckets.astype(jnp.float32)
    dof = grad_out.astype(jnp.float32)
    kept, causal = causal_scores(query, key)
    local = jnp.einsum('hts,she->the', kept, vf)
    first = coef[0].T[:, :, None]
    reads = jnp.einsum('the,lhef->lthf', qf, bf)
    grad_first = lax.optimization_barrier(jnp.sum(dof * local, axis=-1))
    grad_rest = lax.optimization_barrier(jnp.sum(dof[None] * reads, axis=-1))
    grad_coef = jnp.concatenate([grad_first.T[None], grad_rest.transpose(0, 2, 1)], axis=0)
    weighted = (first * dof).astype(jnp.bfloat16).astype(jnp.float32)
    grad_value = jnp.einsum('hts,the->she', kept, weighted)
    pair = jnp.einsum('the,she->hts', dof, vf) * coef[0][:, :, None]
    pair = jnp.where(causal[None], pair, 0.0).astype(jnp.bfloat16).astype(jnp.float32)
    grad_query = jnp.einsum('hts,she->the', pair, kf)
    grad_key = jnp.einsum('hts,the->she', pair, qf)
    scaled = (coef[1:].transpose(0, 2, 1)[..., None] * dof[None]).astype(jnp.bfloat16).astype(jnp.float32)
    grad_query = grad_query + jnp.einsum('lthf,lhef->the', scaled, bf)
    grad_buckets = jnp.einsum('the,lthf->lhef', qf, scaled)
    return (grad_query, grad_key, grad_value, grad_coef, grad_buckets)

def reference(query, key, value, level_coef, gain, cotangent):
    count = N_SEQ
    size = TOK_DEV
    shape4 = (count, size, HEADS, HEAD_DIM)
    q4 = query.reshape(shape4)
    k4 = key.reshape(shape4)
    v4 = value.reshape(shape4)
    c4 = cotangent.reshape(shape4)
    coef = level_coef.reshape(LEVELS, HEADS, count, size).transpose(2, 0, 1, 3)
    states = jnp.einsum('ncha,nchb->nhab', k4.astype(jnp.float32), v4.astype(jnp.float32))
    groups = jnp.arange(count, dtype=jnp.int32)
    found = []
    for level in range(LEVELS - 1):
        bit = (groups // 2 ** level % 2).astype(jnp.float32)
        found.append(bit[:, None, None, None] * sibling_sums(states, level))
    bucket_half = jnp.stack(found, axis=1).astype(jnp.bfloat16)
    output = lax.map(lambda parts: forward_group(*parts), (q4, k4, v4, coef, bucket_half))
    total = lax.optimization_barrier(jnp.mean(output * output, axis=(2, 3)))
    root = jnp.sqrt(total + EPS)[..., None, None]
    normed = output / root
    gain2 = gain.reshape(HEADS, HEAD_DIM)
    mixed = (normed * gain2).astype(jnp.bfloat16).reshape(TOKENS, HEADS * HEAD_DIM)
    cot = c4.astype(jnp.float32)
    grad_gain = lax.optimization_barrier(jnp.sum(cot * normed, axis=(0, 1))).reshape(-1)
    scaled = cot * gain2
    inner = lax.optimization_barrier(jnp.sum(scaled * output, axis=(2, 3)))[..., None, None]
    grad_out = ((scaled - output * inner / (HEADS * HEAD_DIM * root * root)) / root).astype(jnp.bfloat16)
    q_grad, k_grad, v_grad, coef_grad, bucket_grad = lax.map(lambda parts: backward_group(*parts), (q4, k4, v4, coef, bucket_half, grad_out))
    carried = jnp.zeros_like(states)
    for level in range(LEVELS - 1):
        bit = (groups // 2 ** level % 2).astype(jnp.float32)
        carried = carried + sibling_sums(bit[:, None, None, None] * bucket_grad[:, level], level)
    grad_states = carried.astype(jnp.bfloat16).astype(jnp.float32)
    k_grad = k_grad + jnp.einsum('nshb,nhab->nsha', v4.astype(jnp.float32), grad_states)
    v_grad = v_grad + jnp.einsum('nsha,nhab->nshb', k4.astype(jnp.float32), grad_states)
    flat = (TOKENS, HEADS * HEAD_DIM)
    grad_query = q_grad.astype(jnp.bfloat16).reshape(flat)
    grad_key = k_grad.astype(jnp.bfloat16).reshape(flat)
    grad_value = v_grad.astype(jnp.bfloat16).reshape(flat)
    grad_level = coef_grad.transpose(1, 2, 0, 3).reshape(LEVELS, HEADS, TOKENS)
    return (mixed, grad_query, grad_key, grad_value, grad_level, grad_gain)
```

```python
import functools

import jax
import jax.numpy as jnp
from jax import lax
from jax.experimental import pallas as pl
from jax.experimental.pallas import tpu as pltpu
from jax.sharding import PartitionSpec as P

EPS = 1e-06
F32 = jnp.float32
BF16 = jnp.bfloat16
TILE = 256


def dot(left, right, left_dim, right_dim):
    return lax.dot_general(
        left, right, (((left_dim,), (right_dim,)), ((), ())), preferred_element_type=F32
    )


def lane_sums(block):
    high = block.astype(BF16)
    low = (block - high.astype(F32)).astype(BF16)
    ones = jnp.ones((8, 2 * block.shape[1]), BF16)
    return dot(ones, jnp.concatenate([high, low], axis=1), 1, 1)


def level_columns(coef_ref, head):
    rows = [coef_ref[level, pl.ds(head, 1), :] for level in range(coef_ref.shape[0])]
    rows += [jnp.zeros_like(rows[0])] * (8 - len(rows))
    return jnp.concatenate(rows, axis=0).T


def states_kernel(key_ref, value_ref, out_ref):
    out_ref[0] = dot(key_ref[...], value_ref[...], 0, 0)


def local_kernel(query_ref, key_ref, value_ref, out_ref):
    rows = query_ref.shape[0]
    tile = min(TILE, rows)
    keep = lax.broadcasted_iota(jnp.int32, (tile, tile), 0) >= lax.broadcasted_iota(
        jnp.int32, (tile, tile), 1
    )
    for start in range(0, rows, tile):
        here = query_ref[start : start + tile, :]
        edge = jnp.where(keep, dot(here, key_ref[start : start + tile, :], 1, 1), 0.0)
        total = dot(edge.astype(BF16), value_ref[start : start + tile, :], 1, 0)
        if start:
            full = dot(here, key_ref[:start, :], 1, 1).astype(BF16)
            total += dot(full, value_ref[:start, :], 1, 0)
        out_ref[start : start + tile, :] = total


def output_kernel(
    bits_ref, query_ref, local_ref, cot_ref, gain_ref, coef_ref, *refs
):
    bucket_refs, (out_ref, sums_ref, square_ref, inner_ref) = refs[:-4], refs[-4:]
    head = pl.program_id(0)
    rows = query_ref.shape[0]
    tile = min(TILE, rows)
    columns = level_columns(coef_ref, head)
    width = query_ref.shape[1]
    halves = [
        (ref[0] * bits_ref[level]).astype(BF16) for level, ref in enumerate(bucket_refs)
    ]
    wide = jnp.concatenate(halves, axis=1)

    @pl.when(head == 0)
    def _():
        square_ref[...] = jnp.zeros_like(square_ref)
        inner_ref[...] = jnp.zeros_like(inner_ref)

    for start in range(0, rows, tile):
        span = slice(start, start + tile)
        reads = dot(query_ref[span, :], wide, 1, 0)
        out = columns[span, 0:1] * local_ref[span, :]
        for level in range(len(halves)):
            out += columns[span, level + 1 : level + 2] * reads[:, level * width : (level + 1) * width]
        out_ref[span, :] = out
        weighted = cot_ref[span, :].astype(F32) * gain_ref[...]
        square_ref[span, :] += out * out
        inner_ref[span, :] += weighted * out

    @pl.when(head == pl.num_programs(0) - 1)
    def _():
        sums_ref[0:8, :] = lane_sums(square_ref[...])
        sums_ref[8:16, :] = lane_sums(inner_ref[...])


def grad_output(cot, gain, out, inverse, factor):
    return ((cot * gain - out * factor) * inverse).astype(BF16)


def bucket_kernel(
    bits_ref, query_ref, out_ref, cot_ref, gain_ref, coef_ref, stats_ref, *refs
):
    bucket_refs, (half_ref, gain_out_ref) = refs[:-2], refs[-2:]
    head = pl.program_id(0)
    rows = query_ref.shape[0]
    tile = min(TILE, rows)
    columns = level_columns(coef_ref, head)
    stats = stats_ref[...].T
    totals = [None] * len(bucket_refs)
    gain_total = None
    for start in range(0, rows, tile):
        span = slice(start, start + tile)
        inverse = stats[span, 0:1]
        out = out_ref[span, :]
        cot = cot_ref[span, :].astype(F32)
        part = jnp.sum(cot * (out * inverse), axis=0, keepdims=True)
        gain_total = part if gain_total is None else gain_total + part
        half = grad_output(cot, gain_ref[...], out, inverse, stats[span, 1:2])
        half_ref[span, :] = half
        wide = half.astype(F32)
        scaled = jnp.concatenate(
            [
                (columns[span, level + 1 : level + 2] * wide).astype(BF16)
                for level in range(len(bucket_refs))
            ],
            axis=1,
        )
        part = dot(query_ref[span, :], scaled, 0, 0)
        totals = part if totals[0] is None else totals + part
    width = query_ref.shape[1]
    for level, ref in enumerate(bucket_refs):
        ref[0] = totals[:, level * width : (level + 1) * width] * bits_ref[level]
    gain_out_ref[...] = gain_total[None]


def main_kernel(
    bits_ref,
    query_ref,
    key_ref,
    value_ref,
    local_ref,
    out_ref,
    half_ref,
    gain_ref,
    coef_ref,
    stats_ref,
    *refs,
):
    count = coef_ref.shape[0] - 1
    bucket_refs = refs[:count]
    mixed_ref, grad_query_ref, key_sum_ref, value_sum_ref, level_ref, query_sum_ref = refs[count:]
    head = pl.program_id(0)
    rows, width = query_ref.shape
    tile = min(TILE, rows)
    columns = level_columns(coef_ref, head)
    first_row = coef_ref[0, pl.ds(head, 1), :]
    stats = stats_ref[...].T
    halves = [
        (ref[0] * bits_ref[level]).astype(BF16) for level, ref in enumerate(bucket_refs)
    ]
    wide = jnp.concatenate(halves, axis=1)
    for start in range(0, rows, tile):
        span = slice(start, start + tile)
        mixed_ref[span, :] = (out_ref[span, :] * stats[span, 0:1] * gain_ref[...]).astype(BF16)
        grad = half_ref[span, :].astype(F32)
        reads = dot(query_ref[span, :], wide, 1, 0)
        level_ref[0, pl.ds(head, 1), span] = lane_sums(grad * local_ref[span, :])[0:1]
        for level in range(count):
            read = reads[:, level * width : (level + 1) * width]
            level_ref[level + 1, pl.ds(head, 1), span] = lane_sums(grad * read)[0:1]
        scaled = jnp.concatenate(
            [
                (columns[span, level + 1 : level + 2] * grad).astype(BF16)
                for level in range(count)
            ],
            axis=1,
        )
        query_sum_ref[span, :] = dot(scaled, wide, 1, 1)
    weighted = (columns[:, 0:1] * half_ref[...].astype(F32)).astype(BF16)
    keep = lax.broadcasted_iota(jnp.int32, (tile, tile), 0) <= lax.broadcasted_iota(
        jnp.int32, (tile, tile), 1
    )
    for start in range(0, rows, tile):
        span = slice(start, start + tile)
        key = key_ref[span, :]
        value = value_ref[span, :]
        key_sum = None
        value_sum = None
        for low, high in ((start, start + tile), (start + tile, rows)):
            if low >= high:
                continue
            later = slice(low, high)
            scores = dot(key, query_ref[later, :], 1, 1)
            pair = dot(value, half_ref[later, :], 1, 1) * first_row[:, later]
            if low == start:
                scores = jnp.where(keep, scores, 0.0)
                pair = jnp.where(keep, pair, 0.0)
            scores = scores.astype(BF16)
            pair = pair.astype(BF16)
            value_part = dot(scores, weighted[later, :], 1, 0)
            key_part = dot(pair, query_ref[later, :], 1, 0)
            value_sum = value_part if value_sum is None else value_sum + value_part
            key_sum = key_part if key_sum is None else key_sum + key_part
            query_sum_ref[later, :] += dot(pair, key, 0, 0)
        key_sum_ref[span, :] = key_sum
        value_sum_ref[span, :] = value_sum
    grad_query_ref[...] = query_sum_ref[...].astype(BF16)


def final_kernel(key_ref, value_ref, key_sum_ref, value_sum_ref, state_ref, key_out_ref, value_out_ref):
    state = state_ref[0].astype(BF16)
    key_out_ref[...] = (key_sum_ref[...] + dot(value_ref[...], state, 1, 1)).astype(BF16)
    value_out_ref[...] = (value_sum_ref[...] + dot(key_ref[...], state, 1, 0)).astype(BF16)


def exchange(block, apart, count, direction=None):
    mask = 1 << apart
    route = [(low, low ^ mask) for low in range(count)]
    if direction == "up":
        route = [pair for pair in route if not pair[0] & mask]
    if direction == "down":
        route = [pair for pair in route if pair[0] & mask]
    return lax.ppermute(block, "seq", route)


def body(seq_count, heads_all, query, key, value, level_coef, gain, cotangent):
    rows = query.shape[0]
    heads = level_coef.shape[1]
    width = query.shape[1] // heads
    depth = level_coef.shape[0] - 1
    features = heads_all * query.shape[1]
    group = lax.axis_index("seq")
    bits = jnp.stack([(group // 2**level % 2).astype(F32) for level in range(depth)])
    gain_row = gain.reshape(1, -1)

    smem = pl.BlockSpec(memory_space=pltpu.SMEM)
    token = pl.BlockSpec((rows, width), lambda h: (0, h))
    state = pl.BlockSpec((1, width, width), lambda h: (h, 0, 0))
    gain_spec = pl.BlockSpec((1, width), lambda h: (0, h))
    coef_spec = pl.BlockSpec(level_coef.shape, lambda h: (0, 0, 0))
    stats_spec = pl.BlockSpec((8, rows), lambda h: (0, 0))
    token_f32 = jax.ShapeDtypeStruct((rows, heads * width), F32)
    token_bf16 = jax.ShapeDtypeStruct((rows, heads * width), BF16)
    state_f32 = jax.ShapeDtypeStruct((heads, width, width), F32)
    params = pltpu.CompilerParams(dimension_semantics=("arbitrary",))
    square = rows * width * width * heads

    def call(kernel, name, flops, moved, **keys):
        return pl.pallas_call(
            kernel,
            grid=(heads,),
            name=name,
            compiler_params=params,
            cost_estimate=pl.CostEstimate(flops=flops, bytes_accessed=moved, transcendentals=0),
            **keys,
        )

    size = rows * heads * width
    states = call(
        states_kernel,
        "states",
        2 * square,
        4 * size,
        in_specs=[token, token],
        out_specs=state,
        out_shape=state_f32,
    )(key, value)

    local = call(
        local_kernel,
        "local",
        3 * rows * size,
        10 * size,
        in_specs=[token, token, token],
        out_specs=token,
        out_shape=token_f32,
    )(query, key, value)

    block = states
    buckets = []
    for level in range(depth):
        last = level == depth - 1
        other = exchange(block, level, seq_count, "up" if last else None)
        buckets.append(other)
        if not last:
            block = block + other

    output, sums = call(
        output_kernel,
        "output",
        2 * depth * square,
        12 * size,
        in_specs=[smem, token, token, token, gain_spec, coef_spec] + [state] * depth,
        out_specs=[token, pl.BlockSpec((16, rows), lambda h: (0, 0))],
        out_shape=[token_f32, jax.ShapeDtypeStruct((16, rows), F32)],
        scratch_shapes=[pltpu.VMEM((rows, width), F32)] * 2,
    )(bits, query, local, cotangent, gain_row, level_coef, *buckets)

    total = lax.psum(jnp.stack([sums[0], sums[8]]), "head")
    inverse = lax.rsqrt(total[0] / features + EPS)
    factor = total[1] * inverse * inverse / features
    stats = jnp.concatenate([inverse[None], factor[None], jnp.zeros((6, rows), F32)])

    grads = call(
        bucket_kernel,
        "buckets",
        2 * depth * square,
        10 * size,
        in_specs=[smem, token, token, token, gain_spec, coef_spec, stats_spec],
        out_specs=[state] * depth
        + [token, pl.BlockSpec((1, 1, width), lambda h: (h, 0, 0))],
        out_shape=[state_f32] * depth
        + [token_bf16, jax.ShapeDtypeStruct((heads, 1, width), F32)],
    )(bits, query, output, cotangent, gain_row, level_coef, stats)
    grad_buckets, half, gain_part = grads[:depth], grads[depth], grads[depth + 1]

    carried = None
    for level in reversed(range(depth)):
        if carried is None:
            carried = exchange(grad_buckets[level], level, seq_count, "down")
        else:
            carried = carried + exchange(grad_buckets[level] + carried, level, seq_count)

    grad_gain = gain_part.reshape(-1)
    for level in range(depth):
        grad_gain = grad_gain + exchange(grad_gain, level, seq_count)

    mixed, grad_query, key_sum, value_sum, grad_level = call(
        main_kernel,
        "main",
        8 * rows * size + 4 * depth * square,
        26 * size,
        in_specs=[smem, token, token, token, token, token, token, gain_spec, coef_spec, stats_spec]
        + [state] * depth,
        out_specs=[token, token, token, token, coef_spec],
        out_shape=[
            token_bf16,
            token_bf16,
            token_f32,
            token_f32,
            jax.ShapeDtypeStruct(level_coef.shape, F32),
        ],
        scratch_shapes=[pltpu.VMEM((rows, width), F32)],
    )(bits, query, key, value, local, output, half, gain_row, level_coef, stats, *buckets)

    grad_key, grad_value = call(
        final_kernel,
        "final",
        4 * square,
        16 * size,
        in_specs=[token, token, token, token, state],
        out_specs=[token, token],
        out_shape=[token_bf16, token_bf16],
    )(key, value, key_sum, value_sum, carried)
    return (mixed, grad_query, grad_key, grad_value, grad_level, grad_gain)


def solution(mesh):
    placed = (
        P("seq", "head"),
        P("seq", "head"),
        P("seq", "head"),
        P(None, "head", "seq"),
        P("head"),
        P("seq", "head"),
    )
    return jax.shard_map(
        functools.partial(body, mesh.shape["seq"], mesh.shape["head"]),
        mesh=mesh,
        in_specs=placed,
        out_specs=(
            P("seq", "head"),
            P("seq", "head"),
            P("seq", "head"),
            P("seq", "head"),
            P(None, "head", "seq"),
            P("head"),
        ),
        check_vma=False,
    )
```

```python
import functools

import jax
import jax.numpy as jnp
from jax import lax
from jax.experimental import pallas as pl
from jax.experimental.pallas import tpu as pltpu
from jax.sharding import PartitionSpec as P

EPS = 1e-06
F32 = jnp.float32
BF16 = jnp.bfloat16
TILE = 256
VMEM_LIMIT = 20 * 2**20


def dot(left, right, left_dim, right_dim):
    return lax.dot_general(
        left, right, (((left_dim,), (right_dim,)), ((), ())), preferred_element_type=F32
    )


def lane_sums(block):
    high = block.astype(BF16)
    low = (block - high.astype(F32)).astype(BF16)
    ones = jnp.ones((8, 2 * block.shape[1]), BF16)
    return dot(ones, jnp.concatenate([high, low], axis=1), 1, 1)


def level_columns(coef_ref, head):
    rows = [coef_ref[level, pl.ds(head, 1), :] for level in range(coef_ref.shape[0])]
    rows += [jnp.zeros_like(rows[0])] * (8 - len(rows))
    return jnp.concatenate(rows, axis=0).T


def states_kernel(where_ref, key_ref, value_ref, out_ref):
    out_ref[0] = dot(key_ref[...], value_ref[...], 0, 0)


def local_kernel(where_ref, query_ref, key_ref, value_ref, out_ref):
    rows = query_ref.shape[0]
    tile = min(TILE, rows)
    keep = lax.broadcasted_iota(jnp.int32, (tile, tile), 0) >= lax.broadcasted_iota(
        jnp.int32, (tile, tile), 1
    )
    for start in range(0, rows, tile):
        span = slice(start, start + tile)
        scores = dot(query_ref[start:, :], key_ref[span, :], 1, 1)
        kept = [jnp.where(keep, scores[:tile], 0.0).astype(BF16)]
        if start + tile < rows:
            kept.append(scores[tile:].astype(BF16))
        part = dot(jnp.concatenate(kept, axis=0), value_ref[span, :], 1, 0)
        if start:
            part += out_ref[start:, :]
        out_ref[start:, :] = part


def fill(wide_ref, ref, first, level, bit=None):
    width = ref.shape[1]
    for index in range(ref.shape[0]):
        block = ref[index] if bit is None else ref[index] * bit
        wide_ref[first + index, level * width : (level + 1) * width, :] = block.astype(BF16)


def other_bit(bit, flip):
    return 1 - bit if flip else bit


def output_kernel(where_ref, query_ref, local_ref, cot_ref, gain_ref, coef_ref, *refs):
    bucket_refs, (out_ref, sums_ref, wide_ref) = refs[:-3], refs[-3:]
    heads, _, width = wide_ref.shape
    depth = wide_ref.shape[1] // width

    @pl.when(pl.program_id(0) == 0)
    def _():
        low, high = where_ref[0], where_ref[1]
        half, quarter = heads // 2, heads // 4
        bit = low.astype(F32)
        fill(wide_ref, bucket_refs[0], low * half, 0, bit)
        fill(wide_ref, bucket_refs[1], (1 - low) * half, 0, bit)
        fill(wide_ref, bucket_refs[2], low * half, 1)
        fill(wide_ref, bucket_refs[3], (1 - low) * half, 1)
        for offset in range(4):
            piece = 2 * other_bit(low, offset & 1) + other_bit(high, offset >> 1)
            fill(wide_ref, bucket_refs[4 + offset], piece * quarter, 2)
        for level in range(3, depth):
            fill(wide_ref, bucket_refs[5 + level], 0, level, where_ref[level].astype(F32))

    columns = coef_ref[...].T
    square = None
    for head in range(heads):
        lanes = slice(head * width, (head + 1) * width)
        query = query_ref[:, lanes]
        out = columns[:, head : head + 1] * local_ref[:, lanes]
        for level in range(depth):
            read = dot(query, wide_ref[head, level * width : (level + 1) * width, :], 1, 0)
            place = (level + 1) * heads + head
            out += columns[:, place : place + 1] * read
        out_ref[:, lanes] = out
        weighted = cot_ref[:, lanes].astype(F32) * gain_ref[:, lanes]
        square = out * out if square is None else square + out * out
        inner = weighted * out if head == 0 else inner + weighted * out
    sums_ref[0:1, :] = lane_sums(square)[0:1]
    sums_ref[1:2, :] = lane_sums(inner)[0:1]


def bucket_kernel(features, where_ref, query_ref, out_ref, cot_ref, gain_ref, coef_ref, sums_ref, *refs):
    mixed_ref, half_ref, gain_out_ref = refs[:3]
    mine0_ref, theirs0_ref, mine1_ref, theirs1_ref = refs[3:7]
    quarter_refs, extra_refs, (total_ref, gain_total_ref) = refs[7:11], refs[11:-2], refs[-2:]
    heads, stacked, width = total_ref.shape
    depth = stacked // width
    step = pl.program_id(0)
    tile = query_ref.shape[0]

    @pl.when(step == 0)
    def _():
        total_ref[...] = jnp.zeros_like(total_ref)
        gain_total_ref[...] = jnp.zeros_like(gain_total_ref)

    inverse = lax.rsqrt(sums_ref[0:1, :] / features + EPS)
    factor = sums_ref[1:2, :] * inverse * inverse / features
    columns = jnp.concatenate([inverse, factor, jnp.zeros((6, tile), F32)]).T
    inverse = jnp.broadcast_to(columns[:, 0:1], (tile, width))
    factor = jnp.broadcast_to(columns[:, 1:2], (tile, width))
    for head in range(heads):
        lanes = slice(head * width, (head + 1) * width)
        cot = cot_ref[:, lanes].astype(F32)
        normed = out_ref[:, lanes] * inverse
        gain = gain_ref[:, lanes]
        mixed_ref[:, lanes] = (normed * gain).astype(BF16)
        gain_total_ref[head] += jnp.sum((cot * normed).reshape(tile // 8, 8, width), axis=0)
        half = ((cot * gain) * inverse - normed * factor).astype(BF16)
        half_ref[:, lanes] = half
        turned = query_ref[:, lanes].T.astype(F32)
        stack = jnp.concatenate(
            [
                (turned * coef_ref[(level + 1) * heads + head : (level + 1) * heads + head + 1, :]).astype(BF16)
                for level in range(depth)
            ],
            axis=0,
        )
        total_ref[head] += dot(stack, half, 1, 0)

    @pl.when(step == pl.num_programs(0) - 1)
    def _():
        low, high = where_ref[0], where_ref[1]
        quarter = heads // 4
        for head in range(heads):
            lanes = slice(head * width, (head + 1) * width)
            gain_out_ref[:, lanes] = jnp.sum(gain_total_ref[head], axis=0, keepdims=True)
            piece, inside, place = head // quarter, head % quarter, head % (2 * quarter)
            parts = [
                total_ref[head, level * width : (level + 1) * width, :] * where_ref[level].astype(F32)
                for level in range(depth)
            ]

            @pl.when(low == piece // 2)
            def _():
                mine0_ref[place] = parts[0]
                mine1_ref[place] = parts[1]

            @pl.when(low != piece // 2)
            def _():
                theirs0_ref[place] = parts[0]
                theirs1_ref[place] = parts[1]

            for offset in range(4):
                owner = 2 * other_bit(low, offset & 1) + other_bit(high, offset >> 1)

                @pl.when(owner == piece)
                def _():
                    quarter_refs[offset][inside] = parts[2]

            for level in range(3, depth):
                extra_refs[level - 3][head] = parts[level]


def main_kernel(
    base, where_ref, query_ref, key_ref, value_ref, local_ref, half_ref, coef_ref, wide_ref, *refs
):
    previous, refs = refs[:-7], refs[-7:]
    grad_query_ref, key_sum_ref, value_sum_ref, level_ref, pick_ref, key_acc, value_acc = refs
    levels = coef_ref.shape[0]
    head = base + pl.program_id(0)
    rows, width = query_ref.shape
    tile = min(TILE, rows)

    @pl.when(pl.program_id(0) == 0)
    def _():
        shape = pick_ref.shape
        picked = lax.broadcasted_iota(jnp.int32, shape, 0) // width == lax.broadcasted_iota(
            jnp.int32, shape, 1
        )
        pick_ref[...] = jnp.where(picked, 1.0, 0.0).astype(BF16)
        if previous:
            level_ref[...] = previous[-1][...]

    columns = level_columns(coef_ref, head)
    first_row = coef_ref[0, pl.ds(head, 1), :]
    keep = lax.broadcasted_iota(jnp.int32, (tile, tile), 0) <= lax.broadcasted_iota(
        jnp.int32, (tile, tile), 1
    )
    for start in range(0, rows, tile):
        span = slice(start, start + tile)
        stop = start + tile
        query = query_ref[span, :]
        half = half_ref[span, :]
        grad = half.astype(F32)
        wide_query = query.astype(F32)
        products = [(grad * local_ref[span, :]).astype(BF16)]
        query_sum = None
        for level in range(levels - 1):
            read = dot(half, wide_ref[0, level * width : (level + 1) * width, :], 1, 1)
            products.append((wide_query * read).astype(BF16))
            part = columns[span, level + 1 : level + 2] * read
            query_sum = part if query_sum is None else query_sum + part
        sums = dot(jnp.concatenate(products, axis=1), pick_ref[...], 1, 0).T
        for level in range(levels):
            level_ref[level, pl.ds(head, 1), span] = sums[level : level + 1, :]

        weighted = (columns[span, 0:1] * grad).astype(BF16)
        scores = dot(key_ref[:stop, :], query, 1, 1)
        pair = dot(value_ref[:stop, :], half, 1, 1) * first_row[:, span]
        kept = [jnp.where(keep, scores[start:], 0.0).astype(BF16)]
        pairs = [jnp.where(keep, pair[start:], 0.0).astype(BF16)]
        if start:
            kept = [scores[:start].astype(BF16)] + kept
            pairs = [pair[:start].astype(BF16)] + pairs
        kept = jnp.concatenate(kept, axis=0)
        pairs = jnp.concatenate(pairs, axis=0)
        value_part = dot(kept, weighted, 1, 0)
        key_part = dot(pairs, query, 1, 0)
        if start:
            value_acc[:start, :] += value_part[:start]
            key_acc[:start, :] += key_part[:start]
        value_acc[span, :] = value_part[start:]
        key_acc[span, :] = key_part[start:]
        grad_query_ref[span, :] = (query_sum + dot(pairs, key_ref[:stop, :], 0, 0)).astype(BF16)
    key_sum_ref[...] = key_acc[...]
    value_sum_ref[...] = value_acc[...]


def final_kernel(where_ref, key_ref, value_ref, key_sum_ref, value_sum_ref, own_ref, add_ref, other_ref, *refs):
    extra, (key_out_ref, value_out_ref) = refs[:-2], refs[-2:]
    head = pl.program_id(0)
    half = own_ref.shape[0]
    place = head % half
    mine = head // half == where_ref[0]
    state = jnp.where(mine, own_ref[place] + add_ref[place], other_ref[place])
    if extra:
        state += extra[0][head]
    state = state.astype(BF16)
    key_out_ref[...] = (key_sum_ref[...] + dot(value_ref[...], state, 1, 1)).astype(BF16)
    value_out_ref[...] = (value_sum_ref[...] + dot(key_ref[...], state, 1, 0)).astype(BF16)


def send(block, count, mask, keep=lambda place: True):
    return lax.ppermute(block, "seq", [(g, g ^ mask) for g in range(count) if keep(g)])


def body(count, heads_all, query, key, value, level_coef, gain, cotangent):
    rows = query.shape[0]
    heads = level_coef.shape[1]
    width = query.shape[1] // heads
    depth = level_coef.shape[0] - 1
    features = heads_all * query.shape[1]
    half, quarter = heads // 2, heads // 4
    group = lax.axis_index("seq")
    where = jnp.stack([group // 2**level % 2 for level in range(depth)]).astype(jnp.int32)
    gain_row = gain.reshape(1, -1)
    size = rows * heads * width
    square = size * width

    def spec(shape, at):
        return pl.BlockSpec(shape, at)

    def whole(*shape):
        return pl.BlockSpec(shape, lambda h, where: (0,) * len(shape))

    def shaped(*shape, dtype=F32):
        return jax.ShapeDtypeStruct(shape, dtype)

    def call(kernel, name, grid, flops, moved, in_specs, out_specs, out_shape, scratch=(), aliases=None):
        return pl.pallas_call(
            kernel,
            grid_spec=pltpu.PrefetchScalarGridSpec(
                num_scalar_prefetch=1,
                grid=(grid,),
                in_specs=in_specs,
                out_specs=out_specs,
                scratch_shapes=scratch,
            ),
            out_shape=out_shape,
            name=name,
            input_output_aliases=aliases or {},
            compiler_params=pltpu.CompilerParams(
                dimension_semantics=("arbitrary",), vmem_limit_bytes=VMEM_LIMIT
            ),
            cost_estimate=pl.CostEstimate(flops=flops, bytes_accessed=moved, transcendentals=0),
        )

    def states(mine):
        at = spec(
            (rows, width),
            lambda h, where: (0, h + half * (where[0] if mine else 1 - where[0])),
        )
        return call(
            states_kernel,
            "states",
            half,
            square,
            2 * size,
            [at, at],
            spec((1, width, width), lambda h, where: (h, 0, 0)),
            shaped(half, width, width),
        )(where, key, value)

    def bit(place, level):
        return place >> level & 1

    token = spec((rows, width), lambda h, where: (0, h))
    gain_spec = spec((1, width), lambda h, where: (0, h))
    token_f32 = shaped(rows, heads * width)
    token_bf16 = shaped(rows, heads * width, dtype=BF16)
    coef_spec = whole(*level_coef.shape)
    half_spec = whole(half, width, width)
    quarter_spec = whole(quarter, width, width)
    full_spec = whole(heads, width, width)
    half_f32 = shaped(half, width, width)
    quarter_f32 = shaped(quarter, width, width)
    full_f32 = shaped(heads, width, width)

    theirs = states(False)
    first = send(theirs, count, 1)
    mine = states(True)

    local = call(
        local_kernel,
        "local",
        heads,
        3 * rows * size,
        10 * size,
        [token, token, token],
        token,
        token_f32,
    )(where, query, key, value)

    first_rest = send(mine, count, 1, lambda g: not bit(g, 0))
    pair = mine + first
    second = send(pair, count, 2, lambda g: not bit(g, 1))
    second_rest = send(second, count, 1, lambda g: bit(g, 1))
    four = pair + second
    near = send(four[:quarter], count, 6, lambda g: bit(g, 1) and not bit(g, 2))
    far = send(four[quarter:], count, 4, lambda g: bit(g, 1) and not bit(g, 2))
    third = near + far
    third_rest = [send(third, count, mask, lambda g: bit(g, 2)) for mask in (1, 2, 3)]
    buckets = [first, first_rest, second, second_rest, third] + third_rest
    bucket_specs = [half_spec] * 4 + [quarter_spec] * 4
    if depth > 3:
        low = (where[0] == 0)[None, None, None]
        block = jnp.concatenate([jnp.where(low, mine, theirs), jnp.where(low, theirs, mine)])
        for level in range(3):
            block = block + send(block, count, 1 << level)
        for level in range(3, depth):
            other = send(block, count, 1 << level)
            buckets.append(other)
            bucket_specs.append(full_spec)
            block = block + other

    coef_rows = level_coef.reshape(-1, rows)

    def across(tile):
        return spec((tile, heads * width), lambda h, where: (h, 0))

    def along(count, tile):
        return spec((count, tile), lambda h, where: (0, h))

    tile = min(TILE // 2, rows)
    output, sums, wide = call(
        output_kernel,
        "output",
        rows // tile,
        2 * depth * square,
        12 * size,
        [across(tile)] * 3 + [whole(1, heads * width), along(coef_rows.shape[0], tile)] + bucket_specs,
        [across(tile), along(2, tile), whole(heads, depth * width, width)],
        [token_f32, shaped(2, rows), shaped(heads, depth * width, width, dtype=BF16)],
    )(where, query, local, cotangent, gain_row, coef_rows, *buckets)

    total = lax.psum(sums, "head")

    extra_count = max(depth - 3, 0)
    tile = min(TILE, rows)
    grads = call(
        functools.partial(bucket_kernel, features),
        "buckets",
        rows // tile,
        2 * depth * square,
        10 * size,
        [across(tile)] * 3 + [whole(1, heads * width), along(coef_rows.shape[0], tile), along(2, tile)],
        [across(tile)] * 2
        + [whole(1, heads * width)]
        + [half_spec] * 4
        + [quarter_spec] * 4
        + [full_spec] * extra_count,
        [token_bf16, token_bf16, shaped(1, heads * width)]
        + [half_f32] * 4
        + [quarter_f32] * 4
        + [full_f32] * extra_count,
        [pltpu.VMEM((heads, depth * width, width), F32), pltpu.VMEM((heads, 8, width), F32)],
    )(where, query, output, cotangent, gain_row, coef_rows, total)
    mixed, grad_half, gain_part, mine0, theirs0, mine1, theirs1 = grads[:7]
    quarters, extra = grads[7:11], grads[11:]

    def main(piece, previous):
        base = piece * quarter
        at = spec((rows, width), lambda h, where: (0, base + h))
        ins = [at] * 5 + [
            coef_spec,
            spec((1, depth * width, width), lambda h, where: (base + h, 0, 0)),
        ]
        aliases = {}
        if previous:
            aliases = {1 + len(ins) + index: index for index in range(3)}
            ins += [pl.BlockSpec(memory_space=pl.ANY)] * 3 + [coef_spec]
        return call(
            functools.partial(main_kernel, base),
            "main",
            quarter,
            (8 * rows * size + 4 * depth * square) // 4,
            22 * size // 4,
            ins,
            [at, at, at, coef_spec],
            [token_bf16, token_f32, token_f32, shaped(*level_coef.shape)],
            [pltpu.VMEM(((depth + 1) * width, width), BF16)] + [pltpu.VMEM((rows, width), F32)] * 2,
            aliases,
        )(where, query, key, value, local, grad_half, level_coef, wide, *previous)

    swapped = send(theirs1, count, 1, lambda g: bit(g, 1))
    gathered = quarters[0]
    for mask in (1, 2, 3):
        gathered = gathered + send(quarters[mask], count, mask, lambda g: bit(g, 2))
    near = send(gathered, count, 6, lambda g: bit(g, 2) and not bit(g, 1))
    far = send(gathered, count, 4, lambda g: bit(g, 2) and bit(g, 1))
    four = jnp.concatenate([near, far])
    down = send(four + mine1 + swapped, count, 2, lambda g: bit(g, 1))
    add = send(theirs0, count, 1, lambda g: bit(g, 0))
    own = four + down
    other = send(own + mine0, count, 1)

    grad_gain = gain_part.reshape(-1)
    for level in range(depth):
        grad_gain = grad_gain + send(grad_gain, count, 1 << level)

    carried = []
    if depth > 3:
        block = send(extra[-1], count, 1 << (depth - 1))
        for level in reversed(range(3, depth - 1)):
            block = block + send(extra[level - 3] + block, count, 1 << level)
        for level in reversed(range(3)):
            block = block + send(block, count, 1 << level)
        carried = [block]

    results = []
    for piece in range(4):
        results = main(piece, results)
    grad_query, key_sum, value_sum, grad_level = results

    grad_key, grad_value = call(
        final_kernel,
        "final",
        heads,
        4 * square,
        16 * size,
        [token, token, token, token] + [half_spec] * 3 + [full_spec] * len(carried),
        [token, token],
        [token_bf16, token_bf16],
    )(where, key, value, key_sum, value_sum, own, add, other, *carried)
    return (mixed, grad_query, grad_key, grad_value, grad_level, grad_gain)


def solution(mesh):
    placed = (
        P("seq", "head"),
        P("seq", "head"),
        P("seq", "head"),
        P(None, "head", "seq"),
        P("head"),
        P("seq", "head"),
    )
    return jax.shard_map(
        functools.partial(body, mesh.shape["seq"], mesh.shape["head"]),
        mesh=mesh,
        in_specs=placed,
        out_specs=(
            P("seq", "head"),
            P("seq", "head"),
            P("seq", "head"),
            P("seq", "head"),
            P(None, "head", "seq"),
            P("head"),
        ),
        check_vma=False,
    )
```

```python
import functools

import jax
import jax.numpy as jnp
from jax import lax
from jax.experimental import pallas as pl
from jax.experimental.pallas import tpu as pltpu
from jax.sharding import PartitionSpec as P

EPS = 1e-06
F32 = jnp.float32
BF16 = jnp.bfloat16
TILE = 256
VMEM_LIMIT = 20 * 2**20


def dot(left, right, left_dim, right_dim):
    return lax.dot_general(
        left, right, (((left_dim,), (right_dim,)), ((), ())), preferred_element_type=F32
    )


def lane_sums(block):
    high = block.astype(BF16)
    low = (block - high.astype(F32)).astype(BF16)
    ones = jnp.ones((8, 2 * block.shape[1]), BF16)
    return dot(ones, jnp.concatenate([high, low], axis=1), 1, 1)


def level_columns(coef_ref, head):
    rows = [coef_ref[level, pl.ds(head, 1), :] for level in range(coef_ref.shape[0])]
    rows += [jnp.zeros_like(rows[0])] * (8 - len(rows))
    return jnp.concatenate(rows, axis=0).T


def states_kernel(where_ref, key_ref, value_ref, out_ref):
    out_ref[0] = dot(key_ref[...], value_ref[...], 0, 0)


def local_kernel(base, where_ref, query_ref, key_ref, value_ref, *refs):
    out_ref = refs[-1]
    rows, width = out_ref.shape
    lanes = pl.ds(pl.multiple_of((base + pl.program_id(0)) * width, width), width)
    tile = min(TILE, rows)
    keep = lax.broadcasted_iota(jnp.int32, (tile, tile), 0) >= lax.broadcasted_iota(
        jnp.int32, (tile, tile), 1
    )
    for start in range(0, rows, tile):
        span = slice(start, start + tile)
        scores = dot(query_ref[start:, lanes], key_ref[span, lanes], 1, 1)
        kept = [jnp.where(keep, scores[:tile], 0.0).astype(BF16)]
        if start + tile < rows:
            kept.append(scores[tile:].astype(BF16))
        part = dot(jnp.concatenate(kept, axis=0), value_ref[span, lanes], 1, 0)
        if start:
            part += out_ref[start:, :]
        out_ref[start:, :] = part


def fill(wide_ref, ref, first, level, bit=None):
    width = ref.shape[1]
    for index in range(ref.shape[0]):
        block = ref[index] if bit is None else ref[index] * bit
        wide_ref[first + index, level * width : (level + 1) * width, :] = block.astype(BF16)


def other_bit(bit, flip):
    return 1 - bit if flip else bit


def output_kernel(where_ref, query_ref, local_ref, cot_ref, gain_ref, coef_ref, *refs):
    bucket_refs, (out_ref, sums_ref, wide_ref) = refs[:-3], refs[-3:]
    heads, _, width = wide_ref.shape
    depth = wide_ref.shape[1] // width

    @pl.when(pl.program_id(0) == 0)
    def _():
        low, high = where_ref[0], where_ref[1]
        half, quarter = heads // 2, heads // 4
        bit = low.astype(F32)
        fill(wide_ref, bucket_refs[0], low * half, 0, bit)
        fill(wide_ref, bucket_refs[1], (1 - low) * half, 0, bit)
        fill(wide_ref, bucket_refs[2], low * half, 1)
        fill(wide_ref, bucket_refs[3], (1 - low) * half, 1)
        for offset in range(4):
            piece = 2 * other_bit(low, offset & 1) + other_bit(high, offset >> 1)
            fill(wide_ref, bucket_refs[4 + offset], piece * quarter, 2)
        for level in range(3, depth):
            fill(wide_ref, bucket_refs[5 + level], 0, level, where_ref[level].astype(F32))

    columns = coef_ref[...].T
    tile = out_ref.shape[0]
    span = pl.ds(pl.multiple_of(pl.program_id(0) * tile, tile), tile)
    square = None
    for head in range(heads):
        lanes = slice(head * width, (head + 1) * width)
        query = query_ref[span, lanes]
        out = columns[:, head : head + 1] * local_ref[span, lanes]
        for level in range(depth):
            read = dot(query, wide_ref[head, level * width : (level + 1) * width, :], 1, 0)
            place = (level + 1) * heads + head
            out += columns[:, place : place + 1] * read
        out_ref[:, lanes] = out
        weighted = cot_ref[span, lanes].astype(F32) * gain_ref[:, lanes]
        square = out * out if square is None else square + out * out
        inner = weighted * out if head == 0 else inner + weighted * out
    sums_ref[0:1, :] = lane_sums(square)[0:1]
    sums_ref[1:2, :] = lane_sums(inner)[0:1]


def bucket_kernel(features, where_ref, query_ref, out_ref, cot_ref, gain_ref, coef_ref, sums_ref, *refs):
    mixed_ref, half_ref = refs[:2]
    mine0_ref, theirs0_ref, mine1_ref, theirs1_ref = refs[2:6]
    quarter_refs, extra_refs, (total_ref, gain_total_ref) = refs[6:10], refs[10:-2], refs[-2:]
    heads, stacked, width = total_ref.shape
    depth = stacked // width
    step = pl.program_id(0)
    tile = half_ref.shape[0]
    span = pl.ds(pl.multiple_of(step * tile, tile), tile)

    @pl.when(step == 0)
    def _():
        total_ref[...] = jnp.zeros_like(total_ref)
        gain_total_ref[...] = jnp.zeros_like(gain_total_ref)

    inverse = lax.rsqrt(sums_ref[0:1, :] / features + EPS)
    factor = sums_ref[1:2, :] * inverse * inverse / features
    columns = jnp.concatenate([inverse, factor, jnp.zeros((6, tile), F32)]).T
    inverse = jnp.broadcast_to(columns[:, 0:1], (tile, width))
    factor = jnp.broadcast_to(columns[:, 1:2], (tile, width))
    for head in range(heads):
        lanes = slice(head * width, (head + 1) * width)
        cot = cot_ref[span, lanes].astype(F32)
        normed = out_ref[span, lanes] * inverse
        gain = gain_ref[:, lanes]
        mixed_ref[:, lanes] = (normed * gain).astype(BF16)
        gain_total_ref[head] += jnp.sum((cot * normed).reshape(tile // 8, 8, width), axis=0)
        half = ((cot * gain) * inverse - normed * factor).astype(BF16)
        half_ref[:, lanes] = half
        turned = query_ref[span, lanes].T.astype(F32)
        stack = jnp.concatenate(
            [
                (turned * coef_ref[(level + 1) * heads + head : (level + 1) * heads + head + 1, :]).astype(BF16)
                for level in range(depth)
            ],
            axis=0,
        )
        total_ref[head] += dot(stack, half, 1, 0)

    @pl.when(step == pl.num_programs(0) - 1)
    def _():
        low, high = where_ref[0], where_ref[1]
        quarter = heads // 4
        blocks = quarter * width
        for offset in range(4):
            quarter_refs[offset][blocks:, :] = jnp.zeros_like(quarter_refs[offset][blocks:, :])
        for head in range(heads):
            gain_row = jnp.sum(gain_total_ref[head], axis=0, keepdims=True)
            for offset in range(4):
                quarter_refs[offset][blocks + head : blocks + head + 1, :] = gain_row
            piece, inside, place = head // quarter, head % quarter, head % (2 * quarter)
            parts = [
                total_ref[head, level * width : (level + 1) * width, :] * where_ref[level].astype(F32)
                for level in range(depth)
            ]

            @pl.when(low == piece // 2)
            def _():
                mine0_ref[place] = parts[0]
                mine1_ref[place] = parts[1]

            @pl.when(low != piece // 2)
            def _():
                theirs0_ref[place] = parts[0]
                theirs1_ref[place] = parts[1]

            for offset in range(4):
                owner = 2 * other_bit(low, offset & 1) + other_bit(high, offset >> 1)

                @pl.when(owner == piece)
                def _():
                    quarter_refs[offset][inside * width : (inside + 1) * width, :] = parts[2]

            for level in range(3, depth):
                extra_refs[level - 3][head] = parts[level]


def main_kernel(
    base, where_ref, query_ref, key_ref, value_ref, local_ref, half_ref, coef_ref, wide_ref, *refs
):
    previous, refs = refs[:-7], refs[-7:]
    grad_query_ref, key_sum_ref, value_sum_ref, level_ref, pick_ref, key_acc, value_acc = refs
    levels = coef_ref.shape[0]
    head = base + pl.program_id(0)
    rows, width = key_acc.shape
    lanes = pl.ds(pl.multiple_of(head * width, width), width)
    tile = min(TILE, rows)

    @pl.when(pl.program_id(0) == 0)
    def _():
        shape = pick_ref.shape
        picked = lax.broadcasted_iota(jnp.int32, shape, 0) // width == lax.broadcasted_iota(
            jnp.int32, shape, 1
        )
        pick_ref[...] = jnp.where(picked, 1.0, 0.0).astype(BF16)
        if previous:
            level_ref[...] = previous[-1][...]

    columns = level_columns(coef_ref, head)
    first_row = coef_ref[0, pl.ds(head, 1), :]
    keep = lax.broadcasted_iota(jnp.int32, (tile, tile), 0) <= lax.broadcasted_iota(
        jnp.int32, (tile, tile), 1
    )
    for start in range(0, rows, tile):
        span = slice(start, start + tile)
        stop = start + tile
        query = query_ref[span, lanes]
        half = half_ref[span, lanes]
        grad = half.astype(F32)
        wide_query = query.astype(F32)
        products = [(grad * local_ref[span, lanes]).astype(BF16)]
        query_sum = None
        for level in range(levels - 1):
            read = dot(half, wide_ref[0, level * width : (level + 1) * width, :], 1, 1)
            products.append((wide_query * read).astype(BF16))
            part = columns[span, level + 1 : level + 2] * read
            query_sum = part if query_sum is None else query_sum + part
        sums = dot(jnp.concatenate(products, axis=1), pick_ref[...], 1, 0).T
        for level in range(levels):
            level_ref[level, pl.ds(head, 1), span] = sums[level : level + 1, :]

        weighted = (columns[span, 0:1] * grad).astype(BF16)
        scores = dot(key_ref[:stop, lanes], query, 1, 1)
        pair = dot(value_ref[:stop, lanes], half, 1, 1) * first_row[:, span]
        kept = [jnp.where(keep, scores[start:], 0.0).astype(BF16)]
        pairs = [jnp.where(keep, pair[start:], 0.0).astype(BF16)]
        if start:
            kept = [scores[:start].astype(BF16)] + kept
            pairs = [pair[:start].astype(BF16)] + pairs
        kept = jnp.concatenate(kept, axis=0)
        pairs = jnp.concatenate(pairs, axis=0)
        value_part = dot(kept, weighted, 1, 0)
        key_part = dot(pairs, query, 1, 0)
        if start:
            value_acc[:start, :] += value_part[:start]
            key_acc[:start, :] += key_part[:start]
        value_acc[span, :] = value_part[start:]
        key_acc[span, :] = key_part[start:]
        grad_query_ref[span, :] = (query_sum + dot(pairs, key_ref[:stop, lanes], 0, 0)).astype(BF16)
    key_sum_ref[...] = key_acc[...]
    value_sum_ref[...] = value_acc[...]


def lower_kernel(where_ref, near_ref, far_ref, mine_ref, swapped_ref, out_ref):
    half, width, _ = mine_ref.shape
    quarter = half // 2
    blocks = quarter * width
    for index in range(half):
        source, place = (near_ref, index) if index < quarter else (far_ref, index - quarter)
        rows = slice(index * width, (index + 1) * width)
        out_ref[rows, :] = source[place * width : (place + 1) * width, :] + (
            mine_ref[index] + swapped_ref[index]
        )
    both = where_ref[1] * where_ref[2] == 1
    out_ref[2 * blocks :, :] = jnp.where(both, far_ref[blocks:, :], near_ref[blocks:, :])


def own_kernel(where_ref, near_ref, far_ref, down_ref, mine_ref, sum_ref, lowered_ref, own_ref, send_ref, gain_ref):
    half, width, _ = mine_ref.shape
    quarter = half // 2
    blocks = quarter * width
    for index in range(half):
        source, place = (near_ref, index) if index < quarter else (far_ref, index - quarter)
        own = source[place * width : (place + 1) * width, :] + down_ref[
            index * width : (index + 1) * width, :
        ]
        own_ref[index] = own
        send_ref[index] = own + mine_ref[index]
    kept = where_ref[1] + where_ref[2] > 0
    gain_ref[...] = sum_ref[blocks:, :] + jnp.where(
        kept, lowered_ref[2 * blocks :, :], down_ref[2 * blocks :, :]
    )


def final_kernel(where_ref, key_ref, value_ref, key_sum_ref, value_sum_ref, own_ref, add_ref, other_ref, *refs):
    extra, (key_out_ref, value_out_ref) = refs[:-2], refs[-2:]
    head = pl.program_id(0)
    half, width, _ = own_ref.shape
    place = head % half
    lanes = pl.ds(pl.multiple_of(head * width, width), width)
    mine = head // half == where_ref[0]
    state = jnp.where(mine, own_ref[place] + add_ref[place], other_ref[place])
    if extra:
        state += extra[0][head]
    state = state.astype(BF16)
    key_out_ref[...] = (key_sum_ref[:, lanes] + dot(value_ref[:, lanes], state, 1, 1)).astype(BF16)
    value_out_ref[...] = (value_sum_ref[:, lanes] + dot(key_ref[:, lanes], state, 1, 0)).astype(BF16)


def send(block, count, mask, keep=lambda place: True):
    return lax.ppermute(block, "seq", [(g, g ^ mask) for g in range(count) if keep(g)])


def body(count, heads_all, query, key, value, level_coef, gain, cotangent):
    rows = query.shape[0]
    heads = level_coef.shape[1]
    width = query.shape[1] // heads
    depth = level_coef.shape[0] - 1
    features = heads_all * query.shape[1]
    half, quarter = heads // 2, heads // 4
    group = lax.axis_index("seq")
    where = jnp.stack([group // 2**level % 2 for level in range(depth)]).astype(jnp.int32)
    gain_row = gain.reshape(1, -1)
    size = rows * heads * width
    square = size * width

    def spec(shape, at):
        return pl.BlockSpec(shape, at)

    def whole(*shape):
        return pl.BlockSpec(shape, lambda h, where: (0,) * len(shape))

    def shaped(*shape, dtype=F32):
        return jax.ShapeDtypeStruct(shape, dtype)

    def call(
        kernel, name, grid, flops, moved, in_specs, out_specs, out_shape, scratch=(), aliases=None
    ):
        return pl.pallas_call(
            kernel,
            grid_spec=pltpu.PrefetchScalarGridSpec(
                num_scalar_prefetch=1,
                grid=(grid,),
                in_specs=in_specs,
                out_specs=out_specs,
                scratch_shapes=scratch,
            ),
            out_shape=out_shape,
            name=name,
            input_output_aliases=aliases or {},
            compiler_params=pltpu.CompilerParams(
                dimension_semantics=("arbitrary",), vmem_limit_bytes=VMEM_LIMIT
            ),
            cost_estimate=pl.CostEstimate(flops=flops, bytes_accessed=moved, transcendentals=0),
        )

    def small(kernel, name, operands, out_shape):
        return pl.pallas_call(
            kernel,
            in_specs=[pl.BlockSpec(memory_space=pltpu.SMEM)] + [pl.BlockSpec(memory_space=pltpu.VMEM)] * operands,
            out_specs=jax.tree.map(lambda _: pl.BlockSpec(memory_space=pltpu.VMEM), out_shape),
            out_shape=out_shape,
            name=name,
            compiler_params=pltpu.CompilerParams(vmem_limit_bytes=VMEM_LIMIT),
            cost_estimate=pl.CostEstimate(flops=size, bytes_accessed=size, transcendentals=0),
        )

    def states(mine):
        at = spec(
            (rows, width),
            lambda h, where: (0, h + half * (where[0] if mine else 1 - where[0])),
        )
        return call(
            states_kernel,
            "states",
            half,
            square,
            2 * size,
            [at, at],
            spec((1, width, width), lambda h, where: (h, 0, 0)),
            shaped(half, width, width),
        )(where, key, value)

    resident = pl.BlockSpec(memory_space=pltpu.VMEM)

    def bit(place, level):
        return place >> level & 1

    token = spec((rows, width), lambda h, where: (0, h))
    gain_spec = spec((1, width), lambda h, where: (0, h))
    token_f32 = shaped(rows, heads * width)
    token_bf16 = shaped(rows, heads * width, dtype=BF16)
    coef_spec = whole(*level_coef.shape)
    half_spec = whole(half, width, width)
    quarter_spec = whole(quarter, width, width)
    full_spec = whole(heads, width, width)
    half_f32 = shaped(half, width, width)
    quarter_f32 = shaped(quarter, width, width)
    full_f32 = shaped(heads, width, width)

    def across(tile):
        return spec((tile, heads * width), lambda h, where: (h, 0))

    def along(count, tile):
        return spec((count, tile), lambda h, where: (0, h))

    theirs = states(False)
    first = send(theirs, count, 1)
    mine = states(True)

    def local_part(piece, previous):
        base = piece * half
        at = spec((rows, width), lambda h, where: (0, base + h))
        return call(
            functools.partial(local_kernel, base),
            "local",
            half,
            3 * rows * size // 2,
            10 * size // 2,
            [resident] * 3 + [pl.BlockSpec(memory_space=pl.ANY)] * len(previous),
            at,
            token_f32,
            aliases={4: 0} if previous else {},
        )(where, query, key, value, *previous)

    local = local_part(0, [])
    first_rest = send(mine, count, 1, lambda g: not bit(g, 0))
    pair = mine + first
    second = send(pair, count, 2, lambda g: not bit(g, 1))
    second, local = lax.optimization_barrier((second, local))
    local = local_part(1, [local])
    second_rest = send(second, count, 1, lambda g: bit(g, 1))
    four = pair + second
    near = send(four[:quarter], count, 6, lambda g: bit(g, 1) and not bit(g, 2))
    far = send(four[quarter:], count, 4, lambda g: bit(g, 1) and not bit(g, 2))
    third = near + far
    third_rest = [send(third, count, mask, lambda g: bit(g, 2)) for mask in (1, 2, 3)]
    buckets = [first, first_rest, second, second_rest, third] + third_rest
    bucket_specs = [half_spec] * 4 + [quarter_spec] * 4
    if depth > 3:
        low = (where[0] == 0)[None, None, None]
        block = jnp.concatenate([jnp.where(low, mine, theirs), jnp.where(low, theirs, mine)])
        for level in range(3):
            block = block + send(block, count, 1 << level)
        for level in range(3, depth):
            other = send(block, count, 1 << level)
            buckets.append(other)
            bucket_specs.append(full_spec)
            block = block + other

    coef_rows = level_coef.reshape(-1, rows)

    tile = min(TILE // 2, rows)
    output, sums, wide = call(
        output_kernel,
        "output",
        rows // tile,
        2 * depth * square,
        12 * size,
        [resident] * 3 + [whole(1, heads * width), along(coef_rows.shape[0], tile)] + bucket_specs,
        [across(tile), along(2, tile), whole(heads, depth * width, width)],
        [token_f32, shaped(2, rows), shaped(heads, depth * width, width, dtype=BF16)],
    )(where, query, local, cotangent, gain_row, coef_rows, *buckets)

    total = sums
    step = 1
    while step < heads_all:
        total = total + lax.ppermute(total, "head", [(g, g ^ step) for g in range(heads_all)])
        step *= 2

    extra_count = max(depth - 3, 0)
    blocks = quarter * width
    carrying = (blocks + -(-heads // 8) * 8, width)
    tile = min(TILE, rows)
    grads = call(
        functools.partial(bucket_kernel, features),
        "buckets",
        rows // tile,
        2 * depth * square,
        10 * size,
        [resident] * 3 + [whole(1, heads * width), along(coef_rows.shape[0], tile), along(2, tile)],
        [across(tile)] * 2
        + [half_spec] * 4
        + [whole(*carrying)] * 4
        + [full_spec] * extra_count,
        [token_bf16, token_bf16]
        + [half_f32] * 4
        + [shaped(*carrying)] * 4
        + [full_f32] * extra_count,
        [pltpu.VMEM((heads, depth * width, width), F32), pltpu.VMEM((heads, 8, width), F32)],
    )(where, query, output, cotangent, gain_row, coef_rows, total)
    mixed, grad_half, mine0, theirs0, mine1, theirs1 = grads[:6]
    quarters, extra = grads[6:10], grads[10:]

    def main(piece, previous):
        base = piece * quarter
        at = spec((rows, width), lambda h, where: (0, base + h))
        ins = [resident] * 5 + [
            coef_spec,
            spec((1, depth * width, width), lambda h, where: (base + h, 0, 0)),
        ]
        aliases = {}
        if previous:
            aliases = {1 + len(ins) + index: index for index in range(3)}
            ins += [pl.BlockSpec(memory_space=pl.ANY)] * 3 + [coef_spec]
        return list(call(
            functools.partial(main_kernel, base),
            "main",
            quarter,
            (8 * rows * size + 4 * depth * square) // 4,
            22 * size // 4,
            ins,
            [at, at, at, coef_spec],
            [token_bf16, token_f32, token_f32, shaped(*level_coef.shape)],
            [pltpu.VMEM(((depth + 1) * width, width), BF16)] + [pltpu.VMEM((rows, width), F32)] * 2,
            aliases,
        )(where, query, key, value, local, grad_half, level_coef, wide, *previous))

    sent = [send(quarters[mask], count, mask) for mask in (1, 2, 3)]
    swapped = send(theirs1, count, 1, lambda g: bit(g, 1))
    results = main(0, [])
    sent, swapped, results[-1] = lax.optimization_barrier((sent, swapped, results[-1]))
    gathered = (quarters[0] + sent[0]) + (sent[1] + sent[2])
    near = send(gathered, count, 6, lambda g: bit(g, 1) != bit(g, 2))
    far = send(gathered, count, 4, lambda g: bit(g, 1))
    results = main(1, results)
    near, far, results[-1] = lax.optimization_barrier((near, far, results[-1]))
    lowered = small(
        lower_kernel, "lower", 4, shaped(2 * blocks + carrying[0] - blocks, width)
    )(where, near, far, mine1, swapped)
    down = send(lowered, count, 2, lambda g: bit(g, 1))
    add = send(theirs0, count, 1, lambda g: bit(g, 0))
    results = main(2, results)
    down, results[-1] = lax.optimization_barrier((down, results[-1]))
    own, moved, gain_sum = small(
        own_kernel, "own", 6, [half_f32, half_f32, shaped(carrying[0] - blocks, width)]
    )(where, near, far, down, mine0, gathered, lowered)
    other = send(moved, count, 1)
    grad_gain = gain_sum[:heads].reshape(-1)
    for level in range(3, depth):
        grad_gain = grad_gain + send(grad_gain, count, 1 << level)
    results = main(3, results)

    carried = []
    if depth > 3:
        block = send(extra[-1], count, 1 << (depth - 1))
        for level in reversed(range(3, depth - 1)):
            block = block + send(extra[level - 3] + block, count, 1 << level)
        for level in reversed(range(3)):
            block = block + send(block, count, 1 << level)
        carried = [block]

    grad_query, key_sum, value_sum, grad_level = results

    grad_key, grad_value = call(
        final_kernel,
        "final",
        heads,
        4 * square,
        16 * size,
        [resident] * 4 + [half_spec] * 3 + [full_spec] * len(carried),
        [token, token],
        [token_bf16, token_bf16],
    )(where, key, value, key_sum, value_sum, own, add, other, *carried)
    return (mixed, grad_query, grad_key, grad_value, grad_level, grad_gain)


def solution(mesh):
    placed = (
        P("seq", "head"),
        P("seq", "head"),
        P("seq", "head"),
        P(None, "head", "seq"),
        P("head"),
        P("seq", "head"),
    )
    return jax.shard_map(
        functools.partial(body, mesh.shape["seq"], mesh.shape["head"]),
        mesh=mesh,
        in_specs=placed,
        out_specs=(
            P("seq", "head"),
            P("seq", "head"),
            P("seq", "head"),
            P("seq", "head"),
            P(None, "head", "seq"),
            P("head"),
        ),
        check_vma=False,
    )
```

```python
import functools

import jax
import jax.numpy as jnp
from jax import lax
from jax.experimental import pallas as pl
from jax.experimental.pallas import tpu as pltpu
from jax.sharding import PartitionSpec as P

EPS = 1e-06
F32 = jnp.float32
BF16 = jnp.bfloat16
TILE = 256
VMEM_LIMIT = 20 * 2**20


def dot(left, right, left_dim, right_dim):
    return lax.dot_general(
        left, right, (((left_dim,), (right_dim,)), ((), ())), preferred_element_type=F32
    )


def lane_sums(block):
    high = block.astype(BF16)
    low = (block - high.astype(F32)).astype(BF16)
    ones = jnp.ones((8, 2 * block.shape[1]), BF16)
    return dot(ones, jnp.concatenate([high, low], axis=1), 1, 1)


def level_columns(coef_ref, head):
    rows = [coef_ref[level, pl.ds(head, 1), :] for level in range(coef_ref.shape[0])]
    rows += [jnp.zeros_like(rows[0])] * (8 - len(rows))
    return jnp.concatenate(rows, axis=0).T


def states_kernel(where_ref, key_ref, value_ref, out_ref):
    out_ref[0] = dot(key_ref[...], value_ref[...], 0, 0)


def local_kernel(base, where_ref, query_ref, key_ref, value_ref, *refs):
    out_ref = refs[-1]
    rows, width = out_ref.shape
    lanes = pl.ds(pl.multiple_of((base + pl.program_id(0)) * width, width), width)
    tile = min(TILE, rows)
    keep = lax.broadcasted_iota(jnp.int32, (tile, tile), 0) >= lax.broadcasted_iota(
        jnp.int32, (tile, tile), 1
    )
    for start in range(0, rows, tile):
        span = slice(start, start + tile)
        scores = dot(query_ref[start:, lanes], key_ref[span, lanes], 1, 1)
        kept = [jnp.where(keep, scores[:tile], 0.0).astype(BF16)]
        if start + tile < rows:
            kept.append(scores[tile:].astype(BF16))
        part = dot(jnp.concatenate(kept, axis=0), value_ref[span, lanes], 1, 0)
        if start:
            part += out_ref[start:, :]
        out_ref[start:, :] = part


def fill(wide_ref, ref, first, level, bit=None):
    width = ref.shape[1]
    for index in range(ref.shape[0]):
        block = ref[index] if bit is None else ref[index] * bit
        wide_ref[first + index, level * width : (level + 1) * width, :] = block.astype(BF16)


def other_bit(bit, flip):
    return 1 - bit if flip else bit


def output_kernel(where_ref, query_ref, local_ref, cot_ref, gain_ref, coef_ref, *refs):
    bucket_refs, (out_ref, sums_ref, wide_ref) = refs[:-3], refs[-3:]
    heads, _, width = wide_ref.shape
    depth = wide_ref.shape[1] // width

    @pl.when(pl.program_id(0) == 0)
    def _():
        low, high = where_ref[0], where_ref[1]
        half, quarter = heads // 2, heads // 4
        bit = low.astype(F32)
        fill(wide_ref, bucket_refs[0], low * half, 0, bit)
        fill(wide_ref, bucket_refs[1], (1 - low) * half, 0, bit)
        fill(wide_ref, bucket_refs[2], low * half, 1)
        fill(wide_ref, bucket_refs[3], (1 - low) * half, 1)
        for offset in range(4):
            piece = 2 * other_bit(low, offset & 1) + other_bit(high, offset >> 1)
            fill(wide_ref, bucket_refs[4 + offset], piece * quarter, 2)
        for level in range(3, depth):
            fill(wide_ref, bucket_refs[5 + level], 0, level, where_ref[level].astype(F32))

    columns = coef_ref[...].T
    tile = out_ref.shape[0]
    span = pl.ds(pl.multiple_of(pl.program_id(0) * tile, tile), tile)
    square = None
    for head in range(heads):
        lanes = slice(head * width, (head + 1) * width)
        query = query_ref[span, lanes]
        out = columns[:, head : head + 1] * local_ref[span, lanes]
        for level in range(depth):
            read = dot(query, wide_ref[head, level * width : (level + 1) * width, :], 1, 0)
            place = (level + 1) * heads + head
            out += columns[:, place : place + 1] * read
        out_ref[:, lanes] = out
        weighted = cot_ref[span, lanes].astype(F32) * gain_ref[:, lanes]
        square = out * out if square is None else square + out * out
        inner = weighted * out if head == 0 else inner + weighted * out
    sums_ref[0:1, :] = lane_sums(square)[0:1]
    sums_ref[1:2, :] = lane_sums(inner)[0:1]


def bucket_kernel(features, where_ref, query_ref, out_ref, cot_ref, gain_ref, coef_ref, sums_ref, *refs):
    mixed_ref, half_ref = refs[:2]
    mine0_ref, theirs0_ref, mine1_ref, theirs1_ref = refs[2:6]
    quarter_refs, extra_refs, (total_ref, gain_total_ref) = refs[6:10], refs[10:-2], refs[-2:]
    heads, stacked, width = total_ref.shape
    depth = stacked // width
    step = pl.program_id(0)
    tile = half_ref.shape[0]
    span = pl.ds(pl.multiple_of(step * tile, tile), tile)

    @pl.when(step == 0)
    def _():
        total_ref[...] = jnp.zeros_like(total_ref)
        gain_total_ref[...] = jnp.zeros_like(gain_total_ref)

    inverse = lax.rsqrt(sums_ref[0:1, :] / features + EPS)
    factor = sums_ref[1:2, :] * inverse * inverse / features
    columns = jnp.concatenate([inverse, factor, jnp.zeros((6, tile), F32)]).T
    inverse = jnp.broadcast_to(columns[:, 0:1], (tile, width))
    factor = jnp.broadcast_to(columns[:, 1:2], (tile, width))
    for head in range(heads):
        lanes = slice(head * width, (head + 1) * width)
        cot = cot_ref[span, lanes].astype(F32)
        normed = out_ref[span, lanes] * inverse
        gain = gain_ref[:, lanes]
        mixed_ref[:, lanes] = (normed * gain).astype(BF16)
        gain_total_ref[head] += jnp.sum((cot * normed).reshape(tile // 8, 8, width), axis=0)
        half = ((cot * gain) * inverse - normed * factor).astype(BF16)
        half_ref[:, lanes] = half
        turned = query_ref[span, lanes].T.astype(F32)
        stack = jnp.concatenate(
            [
                (turned * coef_ref[(level + 1) * heads + head : (level + 1) * heads + head + 1, :]).astype(BF16)
                for level in range(depth)
            ],
            axis=0,
        )
        total_ref[head] += dot(stack, half, 1, 0)

    @pl.when(step == pl.num_programs(0) - 1)
    def _():
        low, high = where_ref[0], where_ref[1]
        quarter = heads // 4
        blocks = quarter * width
        for offset in range(4):
            quarter_refs[offset][blocks:, :] = jnp.zeros_like(quarter_refs[offset][blocks:, :])
        for head in range(heads):
            gain_row = jnp.sum(gain_total_ref[head], axis=0, keepdims=True)
            for offset in range(4):
                quarter_refs[offset][blocks + head : blocks + head + 1, :] = gain_row
            piece, inside, place = head // quarter, head % quarter, head % (2 * quarter)
            parts = [
                total_ref[head, level * width : (level + 1) * width, :] * where_ref[level].astype(F32)
                for level in range(depth)
            ]

            @pl.when(low == piece // 2)
            def _():
                mine0_ref[place] = parts[0]
                mine1_ref[place] = parts[1]

            @pl.when(low != piece // 2)
            def _():
                theirs0_ref[place] = parts[0]
                theirs1_ref[place] = parts[1]

            for offset in range(4):
                owner = 2 * other_bit(low, offset & 1) + other_bit(high, offset >> 1)

                @pl.when(owner == piece)
                def _():
                    quarter_refs[offset][inside * width : (inside + 1) * width, :] = parts[2]

            for level in range(3, depth):
                extra_refs[level - 3][head] = parts[level]


def main_kernel(
    base, where_ref, query_ref, key_ref, value_ref, local_ref, half_ref, coef_ref, wide_ref, *refs
):
    previous, refs = refs[:-6], refs[-6:]
    grad_query_ref, key_sum_ref, value_sum_ref, level_ref, key_acc, value_acc = refs
    levels = coef_ref.shape[0]
    head = base + pl.program_id(0)
    rows, width = key_acc.shape
    lanes = pl.ds(pl.multiple_of(head * width, width), width)
    tile = min(TILE, rows)

    @pl.when(pl.program_id(0) == 0)
    def _():
        if previous:
            level_ref[...] = previous[-1][...]

    columns = level_columns(coef_ref, head)
    first_row = coef_ref[0, pl.ds(head, 1), :]
    keep = lax.broadcasted_iota(jnp.int32, (tile, tile), 0) <= lax.broadcasted_iota(
        jnp.int32, (tile, tile), 1
    )
    for start in range(0, rows, tile):
        span = slice(start, start + tile)
        stop = start + tile
        query = query_ref[span, lanes]
        half = half_ref[span, lanes]
        grad = half.astype(F32)
        wide_query = query.astype(F32)
        lane = lax.broadcasted_iota(jnp.int32, (tile, width), 1)
        sums = jnp.sum(grad * local_ref[span, lanes], axis=1, keepdims=True)
        sums = jnp.broadcast_to(sums, (tile, width))
        query_sum = None
        for level in range(levels - 1):
            read = dot(half, wide_ref[0, level * width : (level + 1) * width, :], 1, 1)
            part = jnp.sum(wide_query * read, axis=1, keepdims=True)
            sums = jnp.where(lane == level + 1, part, sums)
            part = columns[span, level + 1 : level + 2] * read
            query_sum = part if query_sum is None else query_sum + part
        sums = sums.T
        for level in range(levels):
            level_ref[level, pl.ds(head, 1), span] = sums[level : level + 1, :]

        weighted = (columns[span, 0:1] * grad).astype(BF16)
        scores = dot(key_ref[:stop, lanes], query, 1, 1)
        pair = dot(value_ref[:stop, lanes], half, 1, 1) * first_row[:, span]
        kept = [jnp.where(keep, scores[start:], 0.0).astype(BF16)]
        pairs = [jnp.where(keep, pair[start:], 0.0).astype(BF16)]
        if start:
            kept = [scores[:start].astype(BF16)] + kept
            pairs = [pair[:start].astype(BF16)] + pairs
        kept = jnp.concatenate(kept, axis=0)
        pairs = jnp.concatenate(pairs, axis=0)
        value_part = dot(kept, weighted, 1, 0)
        key_part = dot(pairs, query, 1, 0)
        if start:
            value_acc[:start, :] += value_part[:start]
            key_acc[:start, :] += key_part[:start]
        value_acc[span, :] = value_part[start:]
        key_acc[span, :] = key_part[start:]
        grad_query_ref[span, :] = (query_sum + dot(pairs, key_ref[:stop, lanes], 0, 0)).astype(BF16)
    key_sum_ref[...] = key_acc[...]
    value_sum_ref[...] = value_acc[...]


def lower_kernel(where_ref, near_ref, far_ref, mine_ref, swapped_ref, out_ref):
    half, width, _ = mine_ref.shape
    quarter = half // 2
    blocks = quarter * width
    for index in range(half):
        source, place = (near_ref, index) if index < quarter else (far_ref, index - quarter)
        rows = slice(index * width, (index + 1) * width)
        out_ref[rows, :] = source[place * width : (place + 1) * width, :] + (
            mine_ref[index] + swapped_ref[index]
        )
    both = where_ref[1] * where_ref[2] == 1
    out_ref[2 * blocks :, :] = jnp.where(both, far_ref[blocks:, :], near_ref[blocks:, :])


def own_kernel(where_ref, near_ref, far_ref, down_ref, mine_ref, sum_ref, lowered_ref, own_ref, send_ref, gain_ref):
    half, width, _ = mine_ref.shape
    quarter = half // 2
    blocks = quarter * width
    for index in range(half):
        source, place = (near_ref, index) if index < quarter else (far_ref, index - quarter)
        own = source[place * width : (place + 1) * width, :] + down_ref[
            index * width : (index + 1) * width, :
        ]
        own_ref[index] = own
        send_ref[index] = own + mine_ref[index]
    kept = where_ref[1] + where_ref[2] > 0
    gain_ref[...] = sum_ref[blocks:, :] + jnp.where(
        kept, lowered_ref[2 * blocks :, :], down_ref[2 * blocks :, :]
    )


def final_kernel(where_ref, key_ref, value_ref, key_sum_ref, value_sum_ref, own_ref, add_ref, other_ref, *refs):
    extra, (key_out_ref, value_out_ref) = refs[:-2], refs[-2:]
    head = pl.program_id(0)
    half, width, _ = own_ref.shape
    place = head % half
    lanes = pl.ds(pl.multiple_of(head * width, width), width)
    mine = head // half == where_ref[0]
    state = jnp.where(mine, own_ref[place] + add_ref[place], other_ref[place])
    if extra:
        state += extra[0][head]
    state = state.astype(BF16)
    key_out_ref[...] = (key_sum_ref[:, lanes] + dot(value_ref[:, lanes], state, 1, 1)).astype(BF16)
    value_out_ref[...] = (value_sum_ref[:, lanes] + dot(key_ref[:, lanes], state, 1, 0)).astype(BF16)


def send(block, count, mask, keep=lambda place: True):
    return lax.ppermute(block, "seq", [(g, g ^ mask) for g in range(count) if keep(g)])


def body(count, heads_all, query, key, value, level_coef, gain, cotangent):
    rows = query.shape[0]
    heads = level_coef.shape[1]
    width = query.shape[1] // heads
    depth = level_coef.shape[0] - 1
    features = heads_all * query.shape[1]
    half, quarter = heads // 2, heads // 4
    group = lax.axis_index("seq")
    where = jnp.stack([group // 2**level % 2 for level in range(depth)]).astype(jnp.int32)
    gain_row = gain.reshape(1, -1)
    size = rows * heads * width
    square = size * width

    def spec(shape, at):
        return pl.BlockSpec(shape, at)

    def whole(*shape):
        return pl.BlockSpec(shape, lambda h, where: (0,) * len(shape))

    def shaped(*shape, dtype=F32):
        return jax.ShapeDtypeStruct(shape, dtype)

    def call(kernel, grid, flops, moved, in_specs, out_specs, out_shape, scratch=(), aliases=None):
        return pl.pallas_call(
            kernel,
            grid_spec=pltpu.PrefetchScalarGridSpec(
                num_scalar_prefetch=1,
                grid=(grid,),
                in_specs=in_specs,
                out_specs=out_specs,
                scratch_shapes=scratch,
            ),
            out_shape=out_shape,
            input_output_aliases=aliases or {},
            compiler_params=pltpu.CompilerParams(
                dimension_semantics=("arbitrary",), vmem_limit_bytes=VMEM_LIMIT
            ),
            cost_estimate=pl.CostEstimate(flops=flops, bytes_accessed=moved, transcendentals=0),
        )

    def small(kernel, operands, out_shape):
        return pl.pallas_call(
            kernel,
            in_specs=[pl.BlockSpec(memory_space=pltpu.SMEM)] + [pl.BlockSpec(memory_space=pltpu.VMEM)] * operands,
            out_specs=jax.tree.map(lambda _: pl.BlockSpec(memory_space=pltpu.VMEM), out_shape),
            out_shape=out_shape,
            compiler_params=pltpu.CompilerParams(vmem_limit_bytes=VMEM_LIMIT),
            cost_estimate=pl.CostEstimate(flops=size, bytes_accessed=size, transcendentals=0),
        )

    def states(mine):
        at = spec(
            (rows, width),
            lambda h, where: (0, h + half * (where[0] if mine else 1 - where[0])),
        )
        return call(
            states_kernel,
            half,
            square,
            2 * size,
            [at, at],
            spec((1, width, width), lambda h, where: (h, 0, 0)),
            shaped(half, width, width),
        )(where, key, value)

    resident = pl.BlockSpec(memory_space=pltpu.VMEM)

    def bit(place, level):
        return place >> level & 1

    token = spec((rows, width), lambda h, where: (0, h))
    gain_spec = spec((1, width), lambda h, where: (0, h))
    token_f32 = shaped(rows, heads * width)
    token_bf16 = shaped(rows, heads * width, dtype=BF16)
    coef_spec = whole(*level_coef.shape)
    half_spec = whole(half, width, width)
    quarter_spec = whole(quarter, width, width)
    full_spec = whole(heads, width, width)
    half_f32 = shaped(half, width, width)
    full_f32 = shaped(heads, width, width)

    def across(tile):
        return spec((tile, heads * width), lambda h, where: (h, 0))

    def along(count, tile):
        return spec((count, tile), lambda h, where: (0, h))

    theirs = states(False)
    first = send(theirs, count, 1)
    mine = states(True)

    def local_part(piece, previous):
        base = piece * half
        at = spec((rows, width), lambda h, where: (0, base + h))
        return call(
            functools.partial(local_kernel, base),
            half,
            3 * rows * size // 2,
            10 * size // 2,
            [resident] * 3 + [pl.BlockSpec(memory_space=pl.ANY)] * len(previous),
            at,
            token_f32,
            aliases={4: 0} if previous else {},
        )(where, query, key, value, *previous)

    local = local_part(0, [])
    first_rest = send(mine, count, 1, lambda g: not bit(g, 0))
    pair = mine + first
    second = send(pair, count, 2, lambda g: not bit(g, 1))
    second, local = lax.optimization_barrier((second, local))
    local = local_part(1, [local])
    second_rest = send(second, count, 1, lambda g: bit(g, 1))
    four = pair + second
    near = send(four[:quarter], count, 6, lambda g: bit(g, 1) and not bit(g, 2))
    far = send(four[quarter:], count, 4, lambda g: bit(g, 1) and not bit(g, 2))
    third = near + far
    third_rest = [send(third, count, mask, lambda g: bit(g, 2)) for mask in (1, 2, 3)]
    buckets = [first, first_rest, second, second_rest, third] + third_rest
    bucket_specs = [half_spec] * 4 + [quarter_spec] * 4
    if depth > 3:
        low = (where[0] == 0)[None, None, None]
        block = jnp.concatenate([jnp.where(low, mine, theirs), jnp.where(low, theirs, mine)])
        for level in range(3):
            block = block + send(block, count, 1 << level)
        for level in range(3, depth):
            other = send(block, count, 1 << level)
            buckets.append(other)
            bucket_specs.append(full_spec)
            block = block + other

    coef_rows = level_coef.reshape(-1, rows)

    tile = min(TILE, rows)
    output, sums, wide = call(
        output_kernel,
        rows // tile,
        2 * depth * square,
        12 * size,
        [resident] * 3 + [whole(1, heads * width), along(coef_rows.shape[0], tile)] + bucket_specs,
        [across(tile), along(2, tile), whole(heads, depth * width, width)],
        [token_f32, shaped(2, rows), shaped(heads, depth * width, width, dtype=BF16)],
    )(where, query, local, cotangent, gain_row, coef_rows, *buckets)

    total = sums
    step = 1
    while step < heads_all:
        total = total + lax.ppermute(total, "head", [(g, g ^ step) for g in range(heads_all)])
        step *= 2

    extra_count = max(depth - 3, 0)
    blocks = quarter * width
    carrying = (blocks + -(-heads // 8) * 8, width)
    tile = min(TILE, rows)
    grads = call(
        functools.partial(bucket_kernel, features),
        rows // tile,
        2 * depth * square,
        10 * size,
        [resident] * 3 + [whole(1, heads * width), along(coef_rows.shape[0], tile), along(2, tile)],
        [across(tile)] * 2
        + [half_spec] * 4
        + [whole(*carrying)] * 4
        + [full_spec] * extra_count,
        [token_bf16, token_bf16]
        + [half_f32] * 4
        + [shaped(*carrying)] * 4
        + [full_f32] * extra_count,
        [pltpu.VMEM((heads, depth * width, width), F32), pltpu.VMEM((heads, 8, width), F32)],
    )(where, query, output, cotangent, gain_row, coef_rows, total)
    mixed, grad_half, mine0, theirs0, mine1, theirs1 = grads[:6]
    quarters, extra = grads[6:10], grads[10:]

    def main(piece, previous):
        base = piece * quarter
        at = spec((rows, width), lambda h, where: (0, base + h))
        ins = [resident] * 5 + [
            coef_spec,
            spec((1, depth * width, width), lambda h, where: (base + h, 0, 0)),
        ]
        aliases = {}
        if previous:
            aliases = {1 + len(ins) + index: index for index in range(3)}
            ins += [pl.BlockSpec(memory_space=pl.ANY)] * 3 + [coef_spec]
        return list(call(
            functools.partial(main_kernel, base),
            quarter,
            (8 * rows * size + 4 * depth * square) // 4,
            22 * size // 4,
            ins,
            [at, at, at, coef_spec],
            [token_bf16, token_f32, token_f32, shaped(*level_coef.shape)],
            [pltpu.VMEM((rows, width), F32)] * 2,
            aliases,
        )(where, query, key, value, local, grad_half, level_coef, wide, *previous))

    sent = [send(quarters[mask], count, mask) for mask in (1, 2, 3)]
    results = main(0, [])
    sent, theirs1, results[-1] = lax.optimization_barrier((sent, theirs1, results[-1]))
    gathered = (quarters[0] + sent[0]) + (sent[1] + sent[2])
    near = send(gathered, count, 6, lambda g: bit(g, 1) != bit(g, 2))
    far = send(gathered, count, 4, lambda g: bit(g, 1))
    swapped = send(theirs1, count, 1, lambda g: bit(g, 1))
    results = main(1, results)
    near, far, swapped, results[-1] = lax.optimization_barrier((near, far, swapped, results[-1]))
    lowered = small(
        lower_kernel, 4, shaped(2 * blocks + carrying[0] - blocks, width)
    )(where, near, far, mine1, swapped)
    down = send(lowered, count, 2, lambda g: bit(g, 1))
    add = send(theirs0, count, 1, lambda g: bit(g, 0))
    results = main(2, results)
    down, results[-1] = lax.optimization_barrier((down, results[-1]))
    own, moved, gain_sum = small(
        own_kernel, 6, [half_f32, half_f32, shaped(carrying[0] - blocks, width)]
    )(where, near, far, down, mine0, gathered, lowered)
    other = send(moved, count, 1)
    grad_gain = gain_sum[:heads].reshape(-1)
    for level in range(3, depth):
        grad_gain = grad_gain + send(grad_gain, count, 1 << level)
    results = main(3, results)

    carried = []
    if depth > 3:
        block = send(extra[-1], count, 1 << (depth - 1))
        for level in reversed(range(3, depth - 1)):
            block = block + send(extra[level - 3] + block, count, 1 << level)
        for level in reversed(range(3)):
            block = block + send(block, count, 1 << level)
        carried = [block]

    grad_query, key_sum, value_sum, grad_level = results

    grad_key, grad_value = call(
        final_kernel,
        heads,
        4 * square,
        16 * size,
        [resident] * 4 + [half_spec] * 3 + [full_spec] * len(carried),
        [token, token],
        [token_bf16, token_bf16],
    )(where, key, value, key_sum, value_sum, own, add, other, *carried)
    return (mixed, grad_query, grad_key, grad_value, grad_level, grad_gain)


def staged(count, heads_all, *arrays):
    return body(count, heads_all, *arrays)


def solution(mesh):
    placed = (
        P("seq", "head"),
        P("seq", "head"),
        P("seq", "head"),
        P(None, "head", "seq"),
        P("head"),
        P("seq", "head"),
    )
    return jax.shard_map(
        functools.partial(staged, mesh.shape["seq"], mesh.shape["head"]),
        mesh=mesh,
        in_specs=placed,
        out_specs=(
            P("seq", "head"),
            P("seq", "head"),
            P("seq", "head"),
            P("seq", "head"),
            P(None, "head", "seq"),
            P("head"),
        ),
        check_vma=False,
    )
```
